512 devices in a mesh: dp: 32 (over y_lo, z), ctx: 16 (over y_hi, x, core).
Axes of the slice: x: 4, y: 4 (y_hi: 2, y_lo: 2; y = y_hi * 2 + y_lo), z: 16, core: 2. Of those that a mesh axis runs over, the one named last changes fastest.
Arguments:
- hidden_in: bfloat16 [32, 2048, 5376], P('dp', 'ctx'), may hold values from -30 to 30
- w_qkv: bfloat16 [5376, 512], P('ctx'), may hold values from -1 to 1
- d_attn: bfloat16 [32, 2048, 256], P('dp', 'ctx'), may hold values from -6 to 6
- range_len: int32 [32, 16], P('dp', 'ctx'), may hold values from 96 to 128, as said below
- doc_ids: int32 [32, 2048], P('dp', 'ctx'), may hold values from 0 to 1, never falling along the last dimension, each value on 1 to 1536 neighbouring positions
Outputs:
- d_x: bfloat16 [32, 2048, 5376], P('dp', 'ctx')
- d_w: float32 [5376, 512], P('ctx')
The draws below stay inside these ranges and needn't reach their ends.
Inputs may be any that keep to these rules, and one draw needn't show every extreme that they name: `range_len`: every range holds between 96 and 128 live tokens; in every sequence one range holds exactly 128 and another exactly 96.
All inputs are finite; a program needn't handle non-finite values.
Results may differ from the reference program's by a relative error of at most 0.015.
Values may be sent and summed in bfloat16 or wider, within the bound.
A program may use at most 64 MiB of HBM per device.

```python
import math
import jax
import jax.numpy as jnp
import numpy as np
from jax import lax

D = 5376
HD = 128
WINDOW = 1024
QHEADS = 2
CAP = 128
SEQS = 32
BLOCKS = 16
SLOTS = 2048
QKV = 512
MIN_LEN = 96


def draw_hidden_in(key, part):
    values = jnp.clip(jax.random.normal(key, (SEQS, SLOTS, D), jnp.float32), -6.0, 6.0)
    return values.astype(jnp.bfloat16)


def draw_w_qkv(key, part):
    scale = D ** (-0.5)
    whole = jax.random.normal(jax.random.fold_in(key, 5), (D, QKV), jnp.float32) * scale
    return jnp.clip(whole, -1.0, 1.0).astype(jnp.bfloat16)


def draw_range_len(key, part):
    lengths = jax.random.randint(key, (SEQS, BLOCKS), MIN_LEN, CAP + 1)
    chosen = jax.random.randint(jax.random.fold_in(key, 3), (SEQS, 1), 0, BLOCKS)
    other = (chosen + 1) % BLOCKS
    index = jnp.arange(BLOCKS, dtype=jnp.int32)[None, :]
    lengths = jnp.where(index == chosen, CAP, lengths)
    lengths = jnp.where(index == other, MIN_LEN, lengths)
    return lengths.astype(jnp.int32)


def steps_of(key, dims, cuts, low, largest):
    def one(dim, blocks):
        heights = jax.random.uniform(jax.random.fold_in(jax.random.fold_in(key, 6), dim), (blocks,), jnp.float32, low / len(cuts), largest / len(cuts))
        return jnp.repeat(jnp.exp(heights), dims[dim] // blocks).reshape((-1,) + (1,) * (len(dims) - dim - 1))

    loudness = one(*cuts[0])
    for cut in cuts[1:]:
        loudness = loudness * one(*cut)
    return loudness


def length_profile(amount, total, reach, slope):
    portions = [(1 << 20) // math.isqrt(standing ** slope) + 1 for standing in range(2, amount + 1)]
    surplus, holding = total - reach - (amount - 1), [1] * (amount - 1)
    while surplus > 0:
        candidates = [i for i in range(amount - 1) if holding[i] < reach]
        pool, remaining = sum([portions[i] for i in candidates]), surplus
        for i in candidates:
            addition = min(reach - holding[i], max(1, remaining * portions[i] // pool), surplus)
            holding[i] = holding[i] + addition
            surplus = surplus - addition
    return np.array([reach] + holding)


def ragged(stream_key, amount, total, reach, slope):
    if amount == 2:
        one = jax.random.randint(stream_key, (), max(1, total - reach), min(reach, total - 1) + 1)
        return jnp.stack([one, total - one])
    sizes = jnp.asarray(length_profile(amount, total, reach, slope), jnp.int32)
    twos = (amount - 1) // 2
    donor, receiver = sizes[1:1 + 2 * twos:2], sizes[2:2 + 2 * twos:2]
    slack = jnp.minimum(donor - 1, reach - receiver)
    shifted = jax.random.randint(jax.random.fold_in(stream_key, 1), (twos,), 0, 1 << 20) % (slack + 1)
    sizes = sizes.at[1:1 + 2 * twos:2].set(donor - shifted).at[2:2 + 2 * twos:2].set(receiver + shifted)
    return sizes[jax.random.permutation(jax.random.fold_in(stream_key, 2), amount)]


def centred(stream_key, extent, deviation, reach, shards=(), kind=jnp.bfloat16):
    result = deviation * jax.random.normal(stream_key, extent, jnp.float32)
    if shards:
        result = result * steps_of(stream_key, extent, shards, -0.22, 0.18)
    return jnp.clip(result, -reach, reach).astype(kind)


def setup_inputs(seed: int = 0) -> dict:
    splits = jax.random.split(jax.random.key(seed), 6)
    return {
        "hidden_in": draw_hidden_in(jax.random.fold_in(splits[5], 71), 0),
        "w_qkv": draw_w_qkv(jax.random.fold_in(splits[5], 71), 0),
        "d_attn": centred(splits[2], (SEQS, SLOTS, QHEADS * HD), 1.0, 6.0, ((0, 32), (1, 16))),
        "range_len": draw_range_len(jax.random.fold_in(splits[5], 71), 0),
        "doc_ids": jax.vmap(lambda own: jnp.searchsorted(jnp.cumsum(ragged(own, 2, SLOTS, 3 * SLOTS // 4, 0)), jnp.arange(SLOTS), side="right"))(jax.random.split(splits[4], SEQS)).reshape((SEQS, SLOTS)).astype(jnp.int32),
    }


score_scale = 168.0 ** -0.5
neg_fill = -1.0e30


def rotary_tables(positions, head_size):
    half = head_size // 2
    freqs = 10000.0 ** (-(jnp.arange(half, dtype=jnp.float32) * 2.0) / head_size)
    angles = positions.astype(jnp.float32)[:, None] * freqs[None, :]
    return jnp.cos(angles), jnp.sin(angles)


def rotate(values, cosine, sine, sign):
    half = values.shape[-1] // 2
    first = values[..., :half]
    second = values[..., half:]
    return jnp.concatenate([first * cosine - sign * second * sine, second * cosine + sign * first * sine], axis=-1)


def allowed_pairs(query_meta, key_meta):
    qpos = query_meta[:, 0][:, None]
    kpos = key_meta[:, 0][None, :]
    same_doc = query_meta[:, 1][:, None] == key_meta[:, 1][None, :]
    both_live = (query_meta[:, 2][:, None] == 1) & (key_meta[:, 2][None, :] == 1)
    return both_live & same_doc & (kpos <= qpos) & (qpos - kpos < WINDOW)


def one_sequence(tokens, w_qkv, grads, lengths, docs):
    slot = jnp.arange(SLOTS, dtype=jnp.int32)
    block = slot // CAP
    offset = slot - block * CAP
    starts = (jnp.cumsum(lengths) - lengths).astype(jnp.int32)
    positions = starts[block] + offset
    live = offset < lengths[block]
    meta = jnp.stack([positions, docs.astype(jnp.int32), live.astype(jnp.int32)], axis=1)
    cosine, sine = rotary_tables(positions, HD)
    nq = QHEADS * HD
    proj = jnp.dot(tokens, w_qkv, preferred_element_type=jnp.float32)
    queries = rotate(proj[:, :nq].reshape(SLOTS, QHEADS, HD), cosine[:, None, :], sine[:, None, :], 1.0).astype(jnp.bfloat16)
    keys = rotate(proj[:, nq:nq + HD], cosine, sine, 1.0).astype(jnp.bfloat16)
    values = proj[:, nq + HD:].astype(jnp.bfloat16)
    grad_out = grads.reshape(SLOTS, QHEADS, HD)
    qf = queries.astype(jnp.float32)
    kf = keys.astype(jnp.float32)
    vf = values.astype(jnp.float32)
    gf = grad_out.astype(jnp.float32)
    allowed = allowed_pairs(meta, meta)[None]
    scores = score_scale * jnp.einsum("qhd,kd->hqk", qf, kf)
    dots = jnp.einsum("qhd,kd->hqk", gf, vf)
    top = jnp.max(jnp.where(allowed, scores, neg_fill), axis=2)
    expo = jnp.where(allowed, jnp.exp(scores - top[:, :, None]), 0.0)
    total = jnp.sum(expo, axis=2)
    weighted = jnp.sum(expo * dots, axis=2)
    live_rows = live[None, :]
    safe_total = jnp.where(live_rows, total, 1.0)
    lse = jnp.where(live_rows, top + jnp.log(safe_total), 0.0)
    delta = jnp.where(live_rows, weighted / safe_total, 0.0)
    probs = jnp.where(allowed, jnp.exp(scores - lse[:, :, None]), 0.0)
    mixed = (probs * (dots - delta[:, :, None])).astype(jnp.bfloat16).astype(jnp.float32)
    probs16 = probs.astype(jnp.bfloat16).astype(jnp.float32)
    dq = score_scale * jnp.einsum("hqk,kd->qhd", mixed, kf)
    dk = score_scale * jnp.einsum("hqk,qhd->kd", mixed, qf)
    dv = jnp.einsum("hqk,qhd->kd", probs16, gf)
    dq_pre = rotate(dq, cosine[:, None, :], sine[:, None, :], -1.0).reshape(SLOTS, nq)
    dk_pre = rotate(dk, cosine, sine, -1.0)
    d_proj = jnp.concatenate([dq_pre, dk_pre, dv], axis=1).astype(jnp.bfloat16)
    d_x = jnp.dot(d_proj, w_qkv.T, preferred_element_type=jnp.float32).astype(jnp.bfloat16)
    d_w = jnp.dot(tokens.T, d_proj, preferred_element_type=jnp.float32)
    return d_x, d_w


def reference(hidden_in, w_qkv, d_attn, range_len, doc_ids):
    def step(carry, item):
        tokens, grads, lengths, docs = item
        d_x, d_w = one_sequence(tokens, w_qkv, grads, lengths, docs)
        return carry + d_w, d_x

    start = jnp.zeros((D, QKV), jnp.float32)
    d_w, d_x = lax.scan(step, start, (hidden_in, d_attn, range_len, doc_ids))
    return d_x, d_w
```

```python
import functools

import jax
import jax.numpy as jnp
import numpy as np
from jax import lax
from jax.experimental import pallas as pl
from jax.experimental.pallas import tpu as pltpu
from jax.sharding import PartitionSpec as P

HD = 128
WINDOW = 1024
CAP = 128
D = 5376
QKV = 512
RANGES = 16
CHIPS = 8
ROWS = D // RANGES
WIDE = D // CHIPS
REACH = 11
SLOTS = REACH + 1
DOC_STEP = 4096.0
FAR = 1.0e6
NEG = -1.0e30
SCALE = 168.0 ** (-0.5)
MESH = pl.DeviceIdType.MESH
F32 = jnp.float32
BF16 = jnp.bfloat16


def nt(a, b):
    return lax.dot_general(a, b, (((1,), (1,)), ((), ())), preferred_element_type=F32)


def tn(a, b):
    return lax.dot_general(a, b, (((0,), (0,)), ((), ())), preferred_element_type=F32)


def nn(a, b):
    return jnp.dot(a, b, preferred_element_type=F32)


def kernel(
    zn,
    x_ref, w_ref, g_ref, len_ref, doc_ref, freq_ref,
    dx_ref, dwt_ref,
    meta, keypos, xt, xall, wall, part, projr, acc, qt, qs, gs, gt, kvt, sbuf, dbuf, pbuf, dsbuf,
    dkvs, dkvr, dpt, dxs, dxt, a1s, a1r, tb, a2s, a2r, ub, a3s, a3r, ag,
    meta_s, meta_r, w_s, w_r, x_s, x_r, p_s, p_r, kv_s, kv_r, dk_s, dk_r, dp_s, dp_r, dx_s, dx_r,
    a1_s, a1_r, a2_s, a2_r, a3_s, a3_r, ag_s, ag_r, f_s, f_r,
):
    dp = lax.axis_index("dp")
    ctx = lax.axis_index("ctx")
    zi, yl = dp % zn, dp // zn
    chip, core = ctx // 2, ctx % 2
    rz = 256 // zn

    def at(d, c):
        return {"dp": d, "ctx": c}

    def remote(src, dst, ss, rs, dev):
        return pltpu.make_async_remote_copy(
            src_ref=src, dst_ref=dst, send_sem=ss, recv_sem=rs, device_id=dev, device_id_type=MESH
        )

    def lanes(i):
        return pl.ds(pl.multiple_of(i * 128, 128), 128)

    def chip_at(j):
        return at(dp, ((chip + j) % CHIPS) * 2 + core)

    sibling = at(dp, chip * 2 + (1 - core))
    ypair = at((1 - yl) * zn + zi, ctx)

    def zpeer(j):
        return at(yl * zn + (zi + j) % zn, ctx)

    barrier = pltpu.get_barrier_semaphore()

    def greet_ctx(j, carry):
        pl.semaphore_signal(barrier, inc=1, device_id=at(dp, (ctx + j) % RANGES), device_id_type=MESH)
        return carry

    def greet_z(j, carry):
        pl.semaphore_signal(barrier, inc=1, device_id=zpeer(j), device_id_type=MESH)
        return carry

    lax.fori_loop(1, RANGES, greet_ctx, 0)
    lax.fori_loop(1, zn, greet_z, 0)
    pl.semaphore_signal(barrier, inc=1, device_id=ypair, device_id_type=MESH)

    row = lax.broadcasted_iota(jnp.int32, (8, 128), 0)
    meta[ctx] = jnp.where(
        row == 0,
        jnp.broadcast_to(doc_ref[...], (8, 128)),
        jnp.broadcast_to(len_ref[...], (8, 128)),
    )
    for j in range(1, SLOTS):
        @pl.when(ctx - j < 0)
        def _():
            kvt[:, j * 128 : (j + 1) * 128] = jnp.zeros((256, 128), BF16)

        @pl.when(ctx + j >= RANGES)
        def _():
            dkvr[:, j * 128 : (j + 1) * 128] = jnp.zeros((256, 128), BF16)

    wall[pl.ds(pl.multiple_of(core * ROWS, 16), ROWS), :] = w_ref[...]
    for b in range(D // 128):
        xt[b * 128 : (b + 1) * 128, :] = x_ref[:, b * 128 : (b + 1) * 128].T
    pl.semaphore_wait(barrier, RANGES + zn - 1)

    def own_rows(i, n, mult):
        return pl.ds(pl.multiple_of(i * n, mult), n)

    def meta_copy(j):
        return remote(meta.at[ctx], meta.at[ctx], meta_s.at[j - 1], meta_r.at[j - 1], at(dp, (ctx + j) % RANGES))

    def meta_in(j):
        slot = (ctx + RANGES - j) % RANGES
        return remote(meta.at[slot], meta.at[slot], meta_s.at[j - 1], meta_r.at[j - 1], sibling)

    w_mine = own_rows(core, ROWS, 16)
    w_theirs = own_rows(1 - core, ROWS, 16)
    w_copy = remote(wall.at[w_mine, :], wall.at[w_mine, :], w_s, w_r, sibling)
    w_copy.start()
    x_copies = []
    for j in range(1, CHIPS):
        other = (chip + j) % CHIPS
        copy = remote(
            xt.at[own_rows(other, WIDE, 16), :], xall.at[:, lanes(chip)], x_s.at[j - 1], x_r.at[j - 1], chip_at(j)
        )
        copy.start()
        x_copies.append(copy)

    def meta_start(j, carry):
        meta_copy(j).start()
        return carry

    lax.fori_loop(1, RANGES, meta_start, 0)
    xall[:, lanes(chip)] = xt[own_rows(chip, WIDE, 16), :]

    for h in range(2):
        block = g_ref[:, h * 128 : (h + 1) * 128]
        gs[h * 128 : (h + 1) * 128, :] = block
        gt[:, h * 128 : (h + 1) * 128] = block.T

    remote(wall.at[w_theirs, :], wall.at[w_theirs, :], w_s, w_r, sibling).wait_recv()

    acc[...] = tn(wall[...], xall[:, lanes(chip)])
    p_copies = []
    for j in range(1, CHIPS):
        other = (chip + CHIPS - j) % CHIPS
        remote(
            xt.at[own_rows(other, WIDE, 16), :], xall.at[:, lanes(other)], x_s.at[j - 1], x_r.at[j - 1], chip_at(j)
        ).wait_recv()
        part[j - 1] = tn(wall[...], xall[:, lanes(other)]).astype(BF16)
        copy = remote(
            part.at[j - 1], projr.at[j - 1], p_s.at[j - 1], p_r.at[j - 1], chip_at(CHIPS - j)
        )
        copy.start()
        p_copies.append(copy)

    def meta_wait(j, carry):
        meta_in(j).wait_recv()
        return carry

    lax.fori_loop(1, RANGES, meta_wait, 0)
    lane = lax.broadcasted_iota(jnp.int32, (8, 128), 1).astype(F32)
    begin = jnp.zeros((8, 128), F32)
    for r in range(RANGES):
        doc = jnp.broadcast_to(meta[r, 0:1, :], (8, 128)).astype(F32)
        length = jnp.broadcast_to(meta[r, 1:2, :], (8, 128)).astype(F32)
        keypos[r] = jnp.where(lane < length, begin + lane + DOC_STEP * doc, FAR)
        keypos[RANGES + r] = begin + lane
        begin = begin + length
    angle = freq_ref[...] * jnp.broadcast_to(keypos[RANGES + ctx][0:1, :], (64, 128))
    cosine, sine = jnp.cos(angle), jnp.sin(angle)
    own = jnp.broadcast_to(keypos[ctx][0:1, :], (128, 128)).T
    qpos = jnp.where(own >= 0.5 * FAR, -FAR, own)

    for j in range(1, CHIPS):
        remote(part.at[j - 1], projr.at[j - 1], p_s.at[j - 1], p_r.at[j - 1], chip_at(j)).wait_recv()
    for n in range(4):
        rows = slice(n * 128, (n + 1) * 128)
        total = acc[rows, :]
        for j in range(1, CHIPS):
            total = total + projr[j - 1, rows, :].astype(F32)
        if n < 3:
            u, v = total[:64], total[64:]
            total = jnp.concatenate([u * cosine - v * sine, v * cosine + u * sine], axis=0)
        low = total.astype(BF16)
        if n < 2:
            qt[:, rows] = low
            qs[rows, :] = low.astype(F32).T.astype(BF16)
        else:
            kvt[(n - 2) * 128 : (n - 1) * 128, 0:128] = low

    def kv_copy(j, target):
        return remote(
            kvt.at[:, 0:128], kvt.at[:, j * 128 : (j + 1) * 128], kv_s.at[j - 1], kv_r.at[j - 1], at(dp, target)
        )

    for j in range(1, SLOTS):
        @pl.when(ctx + j < RANGES)
        def _():
            kv_copy(j, ctx + j).start()

    for j in range(1, SLOTS):
        @pl.when(ctx - j >= 0)
        def _():
            kv_copy(j, ctx - j).wait_recv()

    sbuf[...] = nn(qs[...], kvt[0:128, :])
    dbuf[...] = nn(gs[...], kvt[128:256, :])
    kpos = []
    for j in range(SLOTS):
        block = keypos[(ctx + RANGES - j) % RANGES][0:1, :]
        kpos.append(jnp.where(ctx - j >= 0, block, jnp.full((1, 128), FAR, F32)))
    kpos = jnp.concatenate(kpos, axis=1)
    step = 16
    for i in range(256 // step):
        rows = slice(i * step, (i + 1) * step)
        qrow = (i * step) % 128
        gap = qpos[qrow : qrow + step, 0:1] - kpos
        allowed = (gap >= 0.0) & (gap < float(WINDOW))
        s = jnp.where(allowed, sbuf[rows, :] * SCALE, NEG)
        dots = dbuf[rows, :]
        top = jnp.maximum(jnp.max(s, axis=1, keepdims=True), 0.1 * NEG)
        e = jnp.exp(s - top)
        total = jnp.sum(e, axis=1, keepdims=True)
        weighted = jnp.sum(e * dots, axis=1, keepdims=True)
        inverse = 1.0 / jnp.where(total > 0.0, total, 1.0)
        prob = e * inverse
        pbuf[rows, :] = prob.astype(BF16)
        dsbuf[rows, :] = (prob * (dots - weighted * inverse)).astype(BF16)

    dk = nn(qt[...], dsbuf[...]) * SCALE
    dv = nn(gt[...], pbuf[...])
    dkvs[0:128, :] = dk.astype(BF16)
    dkvs[128:256, :] = dv.astype(BF16)
    acc[0:128, :] = dk[:, 0:128]
    acc[128:256, :] = dv[:, 0:128]

    def dk_copy(j, target):
        span = slice(j * 128, (j + 1) * 128)
        return remote(dkvs.at[:, span], dkvr.at[:, span], dk_s.at[j - 1], dk_r.at[j - 1], at(dp, target))

    for j in range(1, SLOTS):
        @pl.when(ctx - j >= 0)
        def _():
            dk_copy(j, ctx - j).start()

    for h in range(2):
        dq = nt(kvt[0:128, :], dsbuf[h * 128 : (h + 1) * 128, :]) * SCALE
        u, v = dq[:64], dq[64:]
        dq = jnp.concatenate([u * cosine + v * sine, v * cosine - u * sine], axis=0)
        dpt[h * 128 : (h + 1) * 128, lanes(chip)] = dq.astype(BF16)

    for j in range(1, SLOTS):
        @pl.when(ctx + j < RANGES)
        def _():
            dk_copy(j, ctx + j).wait_recv()

    dk = acc[0:128, :]
    dv = acc[128:256, :]
    for j in range(1, SLOTS):
        span = slice(j * 128, (j + 1) * 128)
        dk = dk + dkvr[0:128, span].astype(F32)
        dv = dv + dkvr[128:256, span].astype(F32)
    u, v = dk[:64], dk[64:]
    dk = jnp.concatenate([u * cosine + v * sine, v * cosine - u * sine], axis=0)
    dpt[256:384, lanes(chip)] = dk.astype(BF16)
    dpt[384:512, lanes(chip)] = dv.astype(BF16)

    def dp_copy(j, slot, dev):
        return remote(dpt.at[:, lanes(slot)], dpt.at[:, lanes(slot)], dp_s.at[j - 1], dp_r.at[j - 1], dev)

    for j in range(1, CHIPS):
        dp_copy(j, chip, chip_at(j)).start()
    dxt[own_rows(chip, WIDE, 16), :] = nn(wall[...], dpt[:, lanes(chip)]).astype(BF16)
    for j in range(1, CHIPS):
        dp_copy(j, (chip + CHIPS - j) % CHIPS, chip_at(j)).wait_recv()

    a1s[...] = nt(dpt[...], xall[w_theirs, :]).astype(BF16)
    a1_copy = remote(a1s, a1r, a1_s, a1_r, sibling)
    a1_copy.start()
    tb[...] = nt(dpt[...], xall[w_mine, :])
    a1_copy.wait_recv()
    tb[...] = tb[...] + a1r[...].astype(F32)
    a2s[...] = tb[own_rows(1 - yl, 256, 256), :].astype(BF16)
    a2_copy = remote(a2s, a2r, a2_s, a2_r, ypair)
    a2_copy.start()

    dx_copies = []
    for j in range(1, CHIPS):
        other = (chip + j) % CHIPS
        dxs[j - 1] = nn(wall[...], dpt[:, lanes(other)]).astype(BF16)
        copy = remote(
            dxs.at[j - 1], dxt.at[own_rows(chip, WIDE, 16), :], dx_s.at[j - 1], dx_r.at[j - 1], chip_at(j)
        )
        copy.start()
        dx_copies.append(copy)

    a2_copy.wait_recv()
    ub[...] = tb[own_rows(yl, 256, 256), :] + a2r[...].astype(F32)
    a3s[...] = ub[...].astype(BF16)

    def a3_copy(j):
        other = (zi + j) % zn
        return remote(a3s.at[own_rows(other, rz, 16), :], a3r.at[j - 1], a3_s.at[j - 1], a3_r.at[j - 1], zpeer(j))

    def a3_start(j, carry):
        a3_copy(j).start()
        return carry

    def a3_wait(j, carry):
        a3_copy(j).wait_recv()
        return carry + a3r[j - 1].astype(F32)

    lax.fori_loop(1, zn, a3_start, 0)

    for j in range(1, CHIPS):
        other = (chip + CHIPS - j) % CHIPS
        remote(
            dxs.at[j - 1], dxt.at[own_rows(other, WIDE, 16), :], dx_s.at[j - 1], dx_r.at[j - 1], chip_at(j)
        ).wait_recv()
    for b in range(D // 128):
        dx_ref[:, b * 128 : (b + 1) * 128] = dxt[b * 128 : (b + 1) * 128, :].T

    total = lax.fori_loop(1, zn, a3_wait, ub[own_rows(zi, rz, 16), :])
    mine = own_rows(yl * zn + zi, rz, 16)
    ag[mine, :] = total.astype(BF16)

    def ag_copy(j, place, dev):
        span = own_rows(place, rz, 16)
        return remote(ag.at[span, :], ag.at[span, :], ag_s.at[j - 1], ag_r.at[j - 1], dev)

    def f_copy(j, place):
        span = own_rows(place, rz, 16)
        return remote(ag.at[span, :], ag.at[span, :], f_s.at[j], f_r.at[j], ypair)

    def ag_start(j, carry):
        ag_copy(j, yl * zn + zi, zpeer(j)).start()
        return carry

    lax.fori_loop(1, zn, ag_start, 0)
    f_copy(0, yl * zn + zi).start()

    def ag_forward(j, carry):
        place = yl * zn + (zi + zn - j) % zn
        ag_copy(j, place, ypair).wait_recv()
        f_copy(j, place).start()
        return carry

    lax.fori_loop(1, zn, ag_forward, 0)

    def f_wait(j, carry):
        f_copy(j, (1 - yl) * zn + (zi + zn - j) % zn).wait_recv()
        return carry

    lax.fori_loop(0, zn, f_wait, 0)
    dwt_ref[...] = ag[...].astype(F32)

    w_copy.wait_send()
    for copy in x_copies + p_copies + dx_copies:
        copy.wait_send()

    def meta_sent(j, carry):
        meta_copy(j).wait_send()
        return carry

    lax.fori_loop(1, RANGES, meta_sent, 0)
    for j in range(1, SLOTS):
        @pl.when(ctx + j < RANGES)
        def _():
            kv_copy(j, ctx + j).wait_send()

        @pl.when(ctx - j >= 0)
        def _():
            dk_copy(j, ctx - j).wait_send()

    for j in range(1, CHIPS):
        dp_copy(j, chip, chip_at(j)).wait_send()
    a1_copy.wait_send()
    a2_copy.wait_send()

    def z_sent(j, carry):
        a3_copy(j).wait_send()
        ag_copy(j, yl * zn + zi, zpeer(j)).wait_send()
        return carry

    lax.fori_loop(1, zn, z_sent, 0)

    def f_sent(j, carry):
        f_copy(j, yl * zn + (zi + zn - j) % zn).wait_send()
        return carry

    lax.fori_loop(0, zn, f_sent, 0)


def body(zn, hidden_in, w_qkv, d_attn, range_len, doc_ids):
    rz = 256 // zn
    freqs = 10000.0 ** (-(np.arange(64, dtype=np.float64) * 2.0) / HD)
    freqs = jnp.asarray(np.broadcast_to(freqs[:, None], (64, 128)).astype(np.float32))
    vmem = pl.BlockSpec(memory_space=pltpu.VMEM)
    dma = pltpu.SemaphoreType.DMA
    scratch = [
        pltpu.VMEM((RANGES, 8, 128), jnp.int32),
        pltpu.VMEM((2 * RANGES, 8, 128), F32),
        pltpu.VMEM((D, 128), BF16),
        pltpu.VMEM((WIDE, CHIPS * 128), BF16),
        pltpu.VMEM((WIDE, QKV), BF16),
        pltpu.VMEM((CHIPS - 1, QKV, 128), BF16),
        pltpu.VMEM((CHIPS - 1, QKV, 128), BF16),
        pltpu.VMEM((QKV, 128), F32),
        pltpu.VMEM((128, 256), BF16),
        pltpu.VMEM((256, 128), BF16),
        pltpu.VMEM((256, 128), BF16),
        pltpu.VMEM((128, 256), BF16),
        pltpu.VMEM((256, SLOTS * 128), BF16),
        pltpu.VMEM((256, SLOTS * 128), F32),
        pltpu.VMEM((256, SLOTS * 128), F32),
        pltpu.VMEM((256, SLOTS * 128), BF16),
        pltpu.VMEM((256, SLOTS * 128), BF16),
        pltpu.VMEM((256, SLOTS * 128), BF16),
        pltpu.VMEM((256, SLOTS * 128), BF16),
        pltpu.VMEM((QKV, CHIPS * 128), BF16),
        pltpu.VMEM((CHIPS - 1, WIDE, 128), BF16),
        pltpu.VMEM((D, 128), BF16),
        pltpu.VMEM((QKV, ROWS), BF16),
        pltpu.VMEM((QKV, ROWS), BF16),
        pltpu.VMEM((QKV, ROWS), F32),
        pltpu.VMEM((256, ROWS), BF16),
        pltpu.VMEM((256, ROWS), BF16),
        pltpu.VMEM((256, ROWS), F32),
        pltpu.VMEM((256, ROWS), BF16),
        pltpu.VMEM((zn - 1, rz, ROWS), BF16),
        pltpu.VMEM((QKV, ROWS), BF16),
        dma((RANGES - 1,)), dma((RANGES - 1,)),
        dma, dma,
        dma((CHIPS - 1,)), dma((CHIPS - 1,)),
        dma((CHIPS - 1,)), dma((CHIPS - 1,)),
        dma((REACH,)), dma((REACH,)),
        dma((REACH,)), dma((REACH,)),
        dma((CHIPS - 1,)), dma((CHIPS - 1,)),
        dma((CHIPS - 1,)), dma((CHIPS - 1,)),
        dma, dma,
        dma, dma,
        dma((zn - 1,)), dma((zn - 1,)),
        dma((zn - 1,)), dma((zn - 1,)),
        dma((zn,)), dma((zn,)),
    ]
    d_x, d_wt = pl.pallas_call(
        functools.partial(kernel, zn),
        name="block_backward",
        out_shape=(jax.ShapeDtypeStruct((CAP, D), BF16), jax.ShapeDtypeStruct((QKV, ROWS), F32)),
        in_specs=[vmem] * 6,
        out_specs=(vmem, vmem),
        scratch_shapes=scratch,
        compiler_params=pltpu.CompilerParams(
            collective_id=0, has_side_effects=True, vmem_limit_bytes=50 * 1024 * 1024
        ),
    )(hidden_in[0], w_qkv, d_attn[0], range_len, doc_ids, freqs)
    return d_x[None], d_wt.T


def solution(mesh):
    return jax.shard_map(
        functools.partial(body, mesh.shape["dp"] // 2),
        mesh=mesh,
        in_specs=(
            P("dp", "ctx", None),
            P("ctx", None),
            P("dp", "ctx", None),
            P("dp", "ctx"),
            P("dp", "ctx"),
        ),
        out_specs=(P("dp", "ctx", None), P("ctx", None)),
        check_vma=False,
    )
```

```python
import functools

import jax
import jax.numpy as jnp
import numpy as np
from jax import lax
from jax.experimental import pallas as pl
from jax.experimental.pallas import tpu as pltpu
from jax.sharding import PartitionSpec as P

HD = 128
WINDOW = 1024
CAP = 128
D = 5376
QKV = 512
RANGES = 16
CHIPS = 8
ROWS = D // RANGES
WIDE = D // CHIPS
REACH = 11
SLOTS = REACH + 1
DOC_STEP = 4096.0
FAR = 1.0e6
NEG = -1.0e30
SCALE = 168.0 ** (-0.5)
MESH = pl.DeviceIdType.MESH
F32 = jnp.float32
BF16 = jnp.bfloat16


def nt(a, b):
    return lax.dot_general(a, b, (((1,), (1,)), ((), ())), preferred_element_type=F32)


def tn(a, b):
    return lax.dot_general(a, b, (((0,), (0,)), ((), ())), preferred_element_type=F32)


def nn(a, b):
    return jnp.dot(a, b, preferred_element_type=F32)


def kernel(
    zn,
    x_ref, w_ref, g_ref, len_ref, doc_ref, freq_ref,
    dx_ref, dwt_ref,
    xv, gv, lenv, docv, freqv,
    meta, keypos, xt, xall, wall, part, projr, proj, dkv, qt, qs, gs, gt, kvt, sbuf, dbuf, pbuf, dsbuf,
    dkvs, dkvr, dpt, dxs, dxt, a1s, a1r, tb, a2s, a2r, ub, a3s, a3r, u2, b3s, b3r, ag,
    in_s, meta_s, meta_r, w_s, w_r, x_s, x_r, p_s, p_r, kv_s, kv_r, dk_s, dk_r, dp_s, dp_r, dx_s, dx_r,
    a1_s, a1_r, a2_s, a2_r, a3_s, a3_r, b3_s, b3_r, c_s, c_r, d_s, d_r, f_s, f_r,
):
    dp = lax.axis_index("dp")
    ctx = lax.axis_index("ctx")
    zi, yl = dp % zn, dp // zn
    chip, core = ctx // 2, ctx % 2
    nb = 4 if zn == 16 else 2
    na = zn // nb
    za, zb = zi // nb, zi % nb

    def at(d, c):
        return {"dp": d, "ctx": c}

    def remote(src, dst, ss, rs, dev):
        return pltpu.make_async_remote_copy(
            src_ref=src, dst_ref=dst, send_sem=ss, recv_sem=rs, device_id=dev, device_id_type=MESH
        )

    def lanes(i):
        return pl.ds(pl.multiple_of(i * 128, 128), 128)

    def chip_at(j):
        return at(dp, ((chip + j) % CHIPS) * 2 + core)

    sibling = at(dp, chip * 2 + (1 - core))
    ypair = at((1 - yl) * zn + zi, ctx)

    def bpeer(j):
        return at(yl * zn + za * nb + (zb + j) % nb, ctx)

    def apeer(j):
        return at(yl * zn + ((za + j) % na) * nb + zb, ctx)

    pending = []
    barrier = pltpu.get_barrier_semaphore()

    def greet_ctx(j, carry):
        pl.semaphore_signal(barrier, inc=1, device_id=at(dp, (ctx + j) % RANGES), device_id_type=MESH)
        return carry

    loads = [
        pltpu.make_async_copy(x_ref.at[0], xv, in_s.at[0]),
        pltpu.make_async_copy(w_ref, wall.at[pl.ds(pl.multiple_of(core * ROWS, 16), ROWS), :], in_s.at[1]),
        pltpu.make_async_copy(g_ref.at[0], gv, in_s.at[2]),
        pltpu.make_async_copy(len_ref, lenv, in_s.at[3]),
        pltpu.make_async_copy(doc_ref, docv, in_s.at[4]),
        pltpu.make_async_copy(freq_ref, freqv, in_s.at[5]),
    ]
    for load in loads:
        load.start()
    for j in range(1, na):
        pl.semaphore_signal(barrier, inc=1, device_id=apeer(j), device_id_type=MESH)
    for j in range(1, nb):
        pl.semaphore_signal(barrier, inc=1, device_id=bpeer(j), device_id_type=MESH)
    pl.semaphore_signal(barrier, inc=1, device_id=ypair, device_id_type=MESH)
    lax.fori_loop(1, RANGES, greet_ctx, 0)
    for load in loads:
        load.wait()

    row = lax.broadcasted_iota(jnp.int32, (8, 128), 0)
    meta[ctx] = jnp.where(
        row == 0,
        jnp.broadcast_to(docv[...], (8, 128)),
        jnp.broadcast_to(lenv[...], (8, 128)),
    )
    for j in range(1, SLOTS):
        @pl.when(ctx - j < 0)
        def _():
            kvt[:, j * 128 : (j + 1) * 128] = jnp.zeros((256, 128), BF16)

        @pl.when(ctx + j >= RANGES)
        def _():
            dkvr[:, j * 128 : (j + 1) * 128] = jnp.zeros((256, 128), BF16)

    for b in range(D // 128):
        xt[b * 128 : (b + 1) * 128, :] = xv[:, b * 128 : (b + 1) * 128].T
    pl.semaphore_wait(barrier, RANGES + na + nb - 2)

    def own_rows(i, n, mult):
        return pl.ds(pl.multiple_of(i * n, mult), n)

    def meta_copy(j):
        return remote(meta.at[ctx], meta.at[ctx], meta_s.at[j - 1], meta_r.at[j - 1], at(dp, (ctx + j) % RANGES))

    def meta_in(j):
        slot = (ctx + RANGES - j) % RANGES
        return remote(meta.at[slot], meta.at[slot], meta_s.at[j - 1], meta_r.at[j - 1], sibling)

    w_mine = own_rows(core, ROWS, 16)
    w_theirs = own_rows(1 - core, ROWS, 16)
    w_copy = remote(wall.at[w_mine, :], wall.at[w_mine, :], w_s, w_r, sibling)
    w_copy.start()
    pending.append(w_copy.wait_send)
    for j in range(1, CHIPS):
        other = (chip + j) % CHIPS
        copy = remote(
            xt.at[own_rows(other, WIDE, 16), :], xall.at[:, lanes(chip)], x_s.at[j - 1], x_r.at[j - 1], chip_at(j)
        )
        copy.start()
        pending.append(copy.wait_send)

    def meta_start(j, carry):
        meta_copy(j).start()
        return carry

    lax.fori_loop(1, RANGES, meta_start, 0)

    def meta_sent(j, carry):
        meta_copy(j).wait_send()
        return carry

    pending.append(lambda: lax.fori_loop(1, RANGES, meta_sent, 0))
    xall[:, lanes(chip)] = xt[own_rows(chip, WIDE, 16), :]

    for h in range(2):
        block = gv[:, h * 128 : (h + 1) * 128]
        gs[h * 128 : (h + 1) * 128, :] = block
        gt[:, h * 128 : (h + 1) * 128] = block.T

    remote(wall.at[w_theirs, :], wall.at[w_theirs, :], w_s, w_r, sibling).wait_recv()

    proj[...] = tn(xall[:, lanes(chip)], wall[...])
    for j in range(1, CHIPS):
        other = (chip + CHIPS - j) % CHIPS
        remote(
            xt.at[own_rows(other, WIDE, 16), :], xall.at[:, lanes(other)], x_s.at[j - 1], x_r.at[j - 1], chip_at(j)
        ).wait_recv()
        part[j - 1] = tn(xall[:, lanes(other)], wall[...]).astype(BF16)
        copy = remote(
            part.at[j - 1], projr.at[j - 1], p_s.at[j - 1], p_r.at[j - 1], chip_at(CHIPS - j)
        )
        copy.start()
        pending.append(copy.wait_send)

    def meta_wait(j, carry):
        meta_in(j).wait_recv()
        return carry

    lax.fori_loop(1, RANGES, meta_wait, 0)
    lane = lax.broadcasted_iota(jnp.int32, (8, 128), 1).astype(F32)
    begin = jnp.zeros((8, 128), F32)
    for r in range(RANGES):
        doc = jnp.broadcast_to(meta[r, 0:1, :], (8, 128)).astype(F32)
        length = jnp.broadcast_to(meta[r, 1:2, :], (8, 128)).astype(F32)
        keypos[r] = jnp.where(lane < length, begin + lane + DOC_STEP * doc, FAR)
        keypos[RANGES + r] = begin + lane
        begin = begin + length
    angle = freqv[...] * jnp.broadcast_to(keypos[RANGES + ctx][0:1, :], (64, 128))
    cosine, sine = jnp.cos(angle), jnp.sin(angle)
    own = jnp.broadcast_to(keypos[ctx][0:1, :], (128, 128)).T
    qpos = jnp.where(own >= 0.5 * FAR, -FAR, own)

    for j in range(1, CHIPS):
        remote(part.at[j - 1], projr.at[j - 1], p_s.at[j - 1], p_r.at[j - 1], chip_at(j)).wait_recv()
    for n in range(4):
        rows = slice(n * 128, (n + 1) * 128)
        total = proj[:, rows]
        for j in range(1, CHIPS):
            total = total + projr[j - 1, :, rows].astype(F32)
        total = total.T
        if n < 3:
            u, v = total[:64], total[64:]
            total = jnp.concatenate([u * cosine - v * sine, v * cosine + u * sine], axis=0)
        low = total.astype(BF16)
        if n < 2:
            qt[:, rows] = low
            qs[rows, :] = low.astype(F32).T.astype(BF16)
        else:
            kvt[(n - 2) * 128 : (n - 1) * 128, 0:128] = low

    def kv_copy(j, target):
        return remote(
            kvt.at[:, 0:128], kvt.at[:, j * 128 : (j + 1) * 128], kv_s.at[j - 1], kv_r.at[j - 1], at(dp, target)
        )

    for j in range(1, SLOTS):
        @pl.when(ctx + j < RANGES)
        def _():
            kv_copy(j, ctx + j).start()

    def kv_sent():
        for j in range(1, SLOTS):
            @pl.when(ctx + j < RANGES)
            def _():
                kv_copy(j, ctx + j).wait_send()

    pending.append(kv_sent)

    for j in range(1, SLOTS):
        @pl.when(ctx - j >= 0)
        def _():
            kv_copy(j, ctx - j).wait_recv()

    sbuf[...] = nn(qs[...], kvt[0:128, :])
    dbuf[...] = nn(gs[...], kvt[128:256, :])
    kpos = []
    for j in range(SLOTS):
        block = keypos[(ctx + RANGES - j) % RANGES][0:1, :]
        kpos.append(jnp.where(ctx - j >= 0, block, jnp.full((1, 128), FAR, F32)))
    kpos = jnp.concatenate(kpos, axis=1)
    step = 16
    for i in range(256 // step):
        rows = slice(i * step, (i + 1) * step)
        qrow = (i * step) % 128
        gap = qpos[qrow : qrow + step, 0:1] - kpos
        allowed = (gap >= 0.0) & (gap < float(WINDOW))
        s = jnp.where(allowed, sbuf[rows, :] * SCALE, NEG)
        dots = dbuf[rows, :]
        top = jnp.maximum(jnp.max(s, axis=1, keepdims=True), 0.1 * NEG)
        e = jnp.exp(s - top)
        total = jnp.sum(e, axis=1, keepdims=True)
        weighted = jnp.sum(e * dots, axis=1, keepdims=True)
        inverse = 1.0 / jnp.where(total > 0.0, total, 1.0)
        prob = e * inverse
        pbuf[rows, :] = prob.astype(BF16)
        dsbuf[rows, :] = (prob * (dots - weighted * inverse)).astype(BF16)

    dk = nn(qt[...], dsbuf[...]) * SCALE
    dv = nn(gt[...], pbuf[...])
    dkvs[0:128, :] = dk.astype(BF16)
    dkvs[128:256, :] = dv.astype(BF16)
    dkv[0:128, :] = dk[:, 0:128]
    dkv[128:256, :] = dv[:, 0:128]

    def dk_copy(j, target):
        span = slice(j * 128, (j + 1) * 128)
        return remote(dkvs.at[:, span], dkvr.at[:, span], dk_s.at[j - 1], dk_r.at[j - 1], at(dp, target))

    for j in range(1, SLOTS):
        @pl.when(ctx - j >= 0)
        def _():
            dk_copy(j, ctx - j).start()

    def dk_sent():
        for j in range(1, SLOTS):
            @pl.when(ctx - j >= 0)
            def _():
                dk_copy(j, ctx - j).wait_send()

    pending.append(dk_sent)

    for h in range(2):
        dq = nt(kvt[0:128, :], dsbuf[h * 128 : (h + 1) * 128, :]) * SCALE
        u, v = dq[:64], dq[64:]
        dq = jnp.concatenate([u * cosine + v * sine, v * cosine - u * sine], axis=0)
        dpt[h * 128 : (h + 1) * 128, lanes(chip)] = dq.astype(BF16)

    def dp_copy(half, j, slot, dev):
        part_ref = dpt.at[half * 256 : (half + 1) * 256, lanes(slot)]
        return remote(part_ref, part_ref, dp_s.at[half, j - 1], dp_r.at[half, j - 1], dev)

    def dp_send(half):
        for j in range(1, CHIPS):
            copy = dp_copy(half, j, chip, chip_at(j))
            copy.start()
            pending.append(copy.wait_send)

    def dp_wait(half):
        for j in range(1, CHIPS):
            dp_copy(half, j, (chip + CHIPS - j) % CHIPS, chip_at(j)).wait_recv()

    dp_send(0)
    for j in range(1, SLOTS):
        @pl.when(ctx + j < RANGES)
        def _():
            dk_copy(j, ctx + j).wait_recv()

    dk = dkv[0:128, :]
    dv = dkv[128:256, :]
    for j in range(1, SLOTS):
        span = slice(j * 128, (j + 1) * 128)
        dk = dk + dkvr[0:128, span].astype(F32)
        dv = dv + dkvr[128:256, span].astype(F32)
    u, v = dk[:64], dk[64:]
    dk = jnp.concatenate([u * cosine + v * sine, v * cosine - u * sine], axis=0)
    dpt[256:384, lanes(chip)] = dk.astype(BF16)
    dpt[384:512, lanes(chip)] = dv.astype(BF16)

    dp_send(1)

    def sum_rows(half):
        return dpt[half * 256 : (half + 1) * 256, :]

    def one(copy):
        copy.start()
        pending.append(copy.wait_send)

    def a1_copy(half):
        return remote(a1s.at[half], a1r.at[half], a1_s.at[half], a1_r.at[half], sibling)

    def a2_copy(half):
        return remote(a2s.at[half], a2r.at[half], a2_s.at[half], a2_r.at[half], ypair)

    def group(i):
        return pl.ds(i * na, na)

    def a3_copy(half, j):
        src = a3s.at[half, group((zb + j) % nb)]
        return remote(src, a3r.at[half, j - 1], a3_s.at[half, j - 1], a3_r.at[half, j - 1], bpeer(j))

    def b3_copy(half, j):
        src = b3s.at[half, pl.ds((za + j) % na, 1)]
        return remote(src, b3r.at[half, j - 1], b3_s.at[half, j - 1], b3_r.at[half, j - 1], apeer(j))

    def c_copy(half, j, place):
        chunk = ag.at[half, yl, pl.ds(place, 1)]
        return remote(chunk, chunk, c_s.at[half, j - 1], c_r.at[half, j - 1], apeer(j))

    def d_copy(half, j, place):
        chunk = ag.at[half, yl, group(place)]
        return remote(chunk, chunk, d_s.at[half, j - 1], d_r.at[half, j - 1], bpeer(j))

    def f_copy(half, j, side, place):
        chunk = ag.at[half, side, group(place)]
        return remote(chunk, chunk, f_s.at[half, j], f_r.at[half, j], ypair)

    def step1(half):
        a1s[half] = nt(sum_rows(half), xall[w_theirs, :]).astype(BF16)
        one(a1_copy(half))
        tb[half] = nt(sum_rows(half), xall[w_mine, :])

    def step2(half):
        a1_copy(half).wait_recv()
        tb[half] = tb[half] + a1r[half].astype(F32)
        a2s[half] = tb[half, own_rows(1 - yl, 128, 128), :].astype(BF16)
        one(a2_copy(half))

    def step3(half):
        a2_copy(half).wait_recv()
        total = tb[half, own_rows(yl, 128, 128), :] + a2r[half].astype(F32)
        for i in range(16):
            ub[half, i] = total[i * 8 : (i + 1) * 8, :]
            a3s[half, i] = total[i * 8 : (i + 1) * 8, :].astype(BF16)
        for j in range(1, nb):
            one(a3_copy(half, j))

    def step4(half):
        total = ub[half, group(zb)]
        for j in range(1, nb):
            a3_copy(half, j).wait_recv()
            total = total + a3r[half, j - 1].astype(F32)
        u2[half] = total
        b3s[half] = total.astype(BF16)
        for j in range(1, na):
            one(b3_copy(half, j))

    def step5(half):
        total = u2[half, pl.ds(za, 1)]
        for j in range(1, na):
            b3_copy(half, j).wait_recv()
            total = total + b3r[half, j - 1].astype(F32)
        place = zb * na + za
        ag[half, yl, pl.ds(place, 1)] = total.astype(BF16)
        for j in range(1, na):
            one(c_copy(half, j, place))

    def step6(half):
        for j in range(1, na):
            c_copy(half, j, zb * na + (za + na - j) % na).wait_recv()
        for j in range(1, nb):
            one(d_copy(half, j, zb))
        one(f_copy(half, 0, yl, zb))

    def step7(half):
        for j in range(1, nb):
            place = (zb + nb - j) % nb
            d_copy(half, j, place).wait_recv()
            one(f_copy(half, j, yl, place))

    def step8(half):
        for j in range(nb):
            f_copy(half, j, 1 - yl, (zb + nb - j) % nb).wait_recv()
        for side in range(2):
            for i in range(16):
                low = half * 256 + side * 128 + i * 8
                dwt_ref[low : low + 8, :] = ag[half, side, i].astype(F32)

    dp_wait(0)
    step1(0)
    step2(0)
    step3(0)
    dp_wait(1)
    step1(1)
    step2(1)

    for j in range(1, CHIPS):
        other = (chip + j) % CHIPS
        dxs[j - 1] = nn(wall[...], dpt[:, lanes(other)]).astype(BF16)
        one(
            remote(dxs.at[j - 1], dxt.at[own_rows(chip, WIDE, 16), :], dx_s.at[j - 1], dx_r.at[j - 1], chip_at(j))
        )
    step4(0)
    step3(1)
    dxt[own_rows(chip, WIDE, 16), :] = nn(wall[...], dpt[:, lanes(chip)]).astype(BF16)
    step5(0)
    step4(1)
    step6(0)
    step5(1)
    step7(0)
    step6(1)
    for j in range(1, CHIPS):
        other = (chip + CHIPS - j) % CHIPS
        remote(
            dxs.at[j - 1], dxt.at[own_rows(other, WIDE, 16), :], dx_s.at[j - 1], dx_r.at[j - 1], chip_at(j)
        ).wait_recv()
    step7(1)
    for b in range(D // 128):
        dx_ref[:, b * 128 : (b + 1) * 128] = dxt[b * 128 : (b + 1) * 128, :].T
    step8(0)
    step8(1)

    for left in pending:
        left()


def body(zn, hidden_in, w_qkv, d_attn, range_len, doc_ids):
    nb = 4 if zn == 16 else 2
    na = zn // nb
    freqs = 10000.0 ** (-(np.arange(64, dtype=np.float64) * 2.0) / HD)
    freqs = jnp.asarray(np.broadcast_to(freqs[:, None], (64, 128)).astype(np.float32))
    vmem = pl.BlockSpec(memory_space=pltpu.VMEM)
    dma = pltpu.SemaphoreType.DMA
    scratch = [
        pltpu.VMEM((CAP, D), BF16),
        pltpu.VMEM((CAP, 256), BF16),
        pltpu.VMEM((1, 1), jnp.int32),
        pltpu.VMEM((1, 128), jnp.int32),
        pltpu.VMEM((64, 128), F32),
        pltpu.VMEM((RANGES, 8, 128), jnp.int32),
        pltpu.VMEM((2 * RANGES, 8, 128), F32),
        pltpu.VMEM((D, 128), BF16),
        pltpu.VMEM((WIDE, CHIPS * 128), BF16),
        pltpu.VMEM((WIDE, QKV), BF16),
        pltpu.VMEM((CHIPS - 1, CAP, QKV), BF16),
        pltpu.VMEM((CHIPS - 1, CAP, QKV), BF16),
        pltpu.VMEM((CAP, QKV), F32),
        pltpu.VMEM((256, 128), F32),
        pltpu.VMEM((128, 256), BF16),
        pltpu.VMEM((256, 128), BF16),
        pltpu.VMEM((256, 128), BF16),
        pltpu.VMEM((128, 256), BF16),
        pltpu.VMEM((256, SLOTS * 128), BF16),
        pltpu.VMEM((256, SLOTS * 128), F32),
        pltpu.VMEM((256, SLOTS * 128), F32),
        pltpu.VMEM((256, SLOTS * 128), BF16),
        pltpu.VMEM((256, SLOTS * 128), BF16),
        pltpu.VMEM((256, SLOTS * 128), BF16),
        pltpu.VMEM((256, SLOTS * 128), BF16),
        pltpu.VMEM((QKV, CHIPS * 128), BF16),
        pltpu.VMEM((CHIPS - 1, WIDE, 128), BF16),
        pltpu.VMEM((D, 128), BF16),
        pltpu.VMEM((2, 256, ROWS), BF16),
        pltpu.VMEM((2, 256, ROWS), BF16),
        pltpu.VMEM((2, 256, ROWS), F32),
        pltpu.VMEM((2, 128, ROWS), BF16),
        pltpu.VMEM((2, 128, ROWS), BF16),
        pltpu.VMEM((2, 16, 8, ROWS), F32),
        pltpu.VMEM((2, 16, 8, ROWS), BF16),
        pltpu.VMEM((2, nb - 1, na, 8, ROWS), BF16),
        pltpu.VMEM((2, na, 8, ROWS), F32),
        pltpu.VMEM((2, na, 8, ROWS), BF16),
        pltpu.VMEM((2, na - 1, 1, 8, ROWS), BF16),
        pltpu.VMEM((2, 2, 16, 8, ROWS), BF16),
        dma((6,)),
        dma((RANGES - 1,)), dma((RANGES - 1,)),
        dma, dma,
        dma((CHIPS - 1,)), dma((CHIPS - 1,)),
        dma((CHIPS - 1,)), dma((CHIPS - 1,)),
        dma((REACH,)), dma((REACH,)),
        dma((REACH,)), dma((REACH,)),
        dma((2, CHIPS - 1)), dma((2, CHIPS - 1)),
        dma((CHIPS - 1,)), dma((CHIPS - 1,)),
        dma((2,)), dma((2,)),
        dma((2,)), dma((2,)),
        dma((2, nb - 1)), dma((2, nb - 1)),
        dma((2, na - 1)), dma((2, na - 1)),
        dma((2, na - 1)), dma((2, na - 1)),
        dma((2, nb - 1)), dma((2, nb - 1)),
        dma((2, nb)), dma((2, nb)),
    ]
    d_x, d_wt = pl.pallas_call(
        functools.partial(kernel, zn),
        name="block_backward",
        out_shape=(jax.ShapeDtypeStruct((CAP, D), BF16), jax.ShapeDtypeStruct((QKV, ROWS), F32)),
        in_specs=[pl.BlockSpec(memory_space=pltpu.HBM)] * 6,
        out_specs=(vmem, vmem),
        scratch_shapes=scratch,
        compiler_params=pltpu.CompilerParams(
            collective_id=0, has_side_effects=True, vmem_limit_bytes=50 * 1024 * 1024
        ),
    )(hidden_in, w_qkv, d_attn, range_len, doc_ids, freqs)
    return d_x[None], d_wt.T


def solution(mesh):
    return jax.shard_map(
        functools.partial(body, mesh.shape["dp"] // 2),
        mesh=mesh,
        in_specs=(
            P("dp", "ctx", None),
            P("ctx", None),
            P("dp", "ctx", None),
            P("dp", "ctx"),
            P("dp", "ctx"),
        ),
        out_specs=(P("dp", "ctx", None), P("ctx", None)),
        check_vma=False,
    )
```
